512 devices in a mesh: seq: 32 (over x, y, core), head: 16 (over z).
Axes of the slice: x: 4, y: 4, z: 16, core: 2. Of those that a mesh axis runs over, the one named last changes fastest.
Arguments:
- queries: bfloat16 [32768, 4096], P('seq', 'head'), may hold values from -6 to 6
- keys: bfloat16 [32768, 4096], P('seq', 'head'), may hold values from -6 to 6
- values: bfloat16 [32768, 4096], P('seq', 'head'), may hold values from -6 to 6
- out_weight: bfloat16 [4096, 4096], P(None, 'head'), may hold values from -0.09375 to 0.09375
Outputs:
- output: bfloat16 [32768, 4096], P('seq', 'head')
The draws below stay inside these ranges and needn't reach their ends.
All inputs are finite; a program needn't handle non-finite values.
Results may differ from the reference program's by a relative error of at most 0.0058.
Values may be sent and summed in bfloat16 or wider, within the bound.
A program may use at most 64 MiB of HBM per device.

```python
import jax
import jax.numpy as jnp
from jax import lax

HEADS = 32
HD = 128
D = 4096
BLOCK = 1024
TOKENS = 32768


def block_levels(key, extent, split, smallest, top_value):
    level, own = 1.0, jax.random.fold_in(key, 6)
    for dim, parts in split:
        heights = jnp.exp(jax.random.uniform(jax.random.fold_in(own, dim), (parts,), jnp.float32, smallest / len(split), top_value / len(split)))
        level = level * jnp.repeat(heights, extent[dim] // parts).reshape([-1 if axis == dim else 1 for axis in range(len(extent))])
    return level


def centred(own_key, dims, scale, most, pieces=(), held_as=jnp.bfloat16):
    level = block_levels(own_key, dims, pieces, -0.22, 0.18) if pieces else 1.0
    values = jax.random.normal(own_key, dims, jnp.float32) * scale * level
    return jnp.minimum(jnp.maximum(values, -most), most).astype(held_as)


def setup_inputs(seed: int = 0) -> dict:
    seeds = jax.random.split(jax.random.key(seed), 5)
    queries = centred(seeds[0], (TOKENS, D), 1.0, 6.0, ((0, 32), (1, 16)))
    keys = centred(seeds[1], (TOKENS, D), 1.0, 6.0, ((0, 32), (1, 16)))
    values = centred(seeds[2], (TOKENS, D), 1.0, 6.0, ((0, 32), (1, 16)))
    out_weight = centred(seeds[3], (D, D), D ** -0.5, 0.09375, ((1, 16),))
    return dict(queries=queries, keys=keys, values=values, out_weight=out_weight)


def reference(queries, keys, values, out_weight):
    blocks_count = TOKENS // BLOCK
    query_blocks = queries.reshape(blocks_count, BLOCK, HEADS, HD)
    key_blocks = keys.reshape(blocks_count, BLOCK, HEADS, HD)
    value_blocks = values.reshape(blocks_count, BLOCK, HEADS, HD)
    causal = jnp.arange(BLOCK)[:, None] >= jnp.arange(BLOCK)[None, :]

    def advance(kv_state, inputs):
        query_rows = inputs[0].astype(jnp.float32)
        key_rows = inputs[1].astype(jnp.float32)
        value_rows = inputs[2].astype(jnp.float32)
        scores = jnp.einsum('thd,shd->hts', query_rows, key_rows)
        scores = jnp.where(causal[None], scores, 0.0)
        scores = lax.optimization_barrier(scores.astype(jnp.bfloat16)).astype(jnp.float32)
        carried = lax.optimization_barrier(kv_state.astype(jnp.bfloat16)).astype(jnp.float32)
        attended = jnp.einsum('hts,shd->thd', scores, value_rows) + jnp.einsum('thd,hde->the', query_rows, carried)
        normed = attended * lax.rsqrt(lax.optimization_barrier(jnp.mean(attended * attended, -1, keepdims=True)) + 1e-06)
        kv_state = kv_state + jnp.einsum('thd,the->hde', key_rows, value_rows)
        return (kv_state, normed.astype(jnp.bfloat16))
    zero_state = jnp.zeros((HEADS, HD, HD), jnp.float32)
    unused, mixed_heads = lax.scan(advance, zero_state, (query_blocks, key_blocks, value_blocks))
    mixed_heads = mixed_heads.reshape(TOKENS, D)
    return jnp.dot(mixed_heads, out_weight, preferred_element_type=jnp.float32).astype(jnp.bfloat16)
```

```python
import jax
import jax.numpy as jnp
from jax import lax
from jax.experimental import pallas as pl
from jax.experimental.pallas import tpu as pltpu
from jax.sharding import PartitionSpec as P

HD = 128
ROWS = 1024
HALF = 512
WIDE = 256
SUB = 256
RING = 16
SIDE = 4
F32 = jnp.float32
BF16 = jnp.bfloat16


def dot(a, b):
    return jnp.dot(a, b, preferred_element_type=F32)


def remote(src, dst, send, recv, where):
    return pltpu.make_async_remote_copy(
        src_ref=src,
        dst_ref=dst,
        send_sem=send,
        recv_sem=recv,
        device_id=where,
        device_id_type=pl.DeviceIdType.MESH,
    )


def kernel(
    q_hbm, k_hbm, v_hbm, w_hbm, out,
    q, k, v, w, intra, acc, mixed,
    s_own, s_send, s_recv, t_own, t_recv, r_own, r_recv, c_own, c_send, c_recv, c_blk,
    in_sems, pair_send, pair_recv, y_send, y_recv, x_send, x_recv, c_sems,
    ra_send, ra_recv, rb_send, rb_recv, la_send, la_recv, lb_send, lb_recv,
):
    seq, z = lax.axis_index("seq"), lax.axis_index("head")
    core, y, x = seq % 2, (seq // 2) % SIDE, seq // (2 * SIDE)
    partner = {"seq": seq + 1 - 2 * core}
    y_peers = [{"seq": (x * SIDE + (y + d) % SIDE) * 2 + core} for d in range(1, SIDE)]
    x_peers = [{"seq": (((x + d) % SIDE) * SIDE + y) * 2 + core} for d in range(1, SIDE)]
    right = {"head": (z + 1) % RING}
    left = {"head": (z + RING - 1) % RING}

    barrier = pltpu.get_barrier_semaphore()
    everyone = [partner, right, left] + y_peers + x_peers
    for who in everyone:
        pl.semaphore_signal(barrier, inc=1, device_id=who, device_id_type=pl.DeviceIdType.MESH)
    loads = [
        pltpu.make_async_copy(src, dst, in_sems.at[i])
        for i, (src, dst) in enumerate(((k_hbm, k), (v_hbm, v), (q_hbm, q), (w_hbm, w)))
    ]
    for load in loads:
        load.start()
    loads[0].wait()
    loads[1].wait()
    states = lax.dot_general(k[...], v[...], (((0,), (0,)), ((), ())), preferred_element_type=F32)
    first, second = states[:HD, :HD], states[HD:, HD:]
    s_own[...] = jnp.where(core == 0, first, second)
    s_send[...] = jnp.where(core == 0, second, first)
    pl.semaphore_wait(barrier, len(everyone))
    pair = remote(s_send, s_recv, pair_send, pair_recv, partner)
    pair.start()

    def intra_part(head, part):
        cols = pl.ds(head * HD, HD)
        rows = pl.ds(part * SUB, SUB)
        width = (part + 1) * SUB
        scores = lax.dot_general(
            q[rows, cols], k[pl.ds(0, width), cols], (((1,), (1,)), ((), ())),
            preferred_element_type=F32,
        )
        query_at = lax.broadcasted_iota(jnp.int32, (SUB, width), 0) + part * SUB
        key_at = lax.broadcasted_iota(jnp.int32, (SUB, width), 1)
        scores = jnp.where(query_at >= key_at, scores, 0.0).astype(BF16)
        intra[rows, cols] = dot(scores, v[pl.ds(0, width), cols])

    loads[2].wait()
    intra_part(0, 0)
    intra_part(1, 0)

    pair.wait()
    t_own[...] = s_own[...] + s_recv[...]
    y_copies = [
        remote(t_own, t_recv.at[d], y_send.at[d], y_recv.at[d], y_peers[d]) for d in range(3)
    ]
    for copy in y_copies:
        copy.start()
    intra_part(0, 1)
    intra_part(1, 1)
    intra_part(0, 2)
    for copy in y_copies:
        copy.wait()
    prefix = jnp.zeros((HD, HD), F32)
    total = t_own[...]
    for d in range(3):
        piece = t_recv[d]
        total = total + piece
        prefix = prefix + jnp.where(d + 1 <= y, piece, 0.0)
    r_own[...] = total
    x_copies = [
        remote(r_own, r_recv.at[d], x_send.at[d], x_recv.at[d], x_peers[d]) for d in range(3)
    ]
    for copy in x_copies:
        copy.start()
    s_send[...] = prefix
    intra_part(1, 2)
    intra_part(0, 3)
    intra_part(1, 3)
    for copy in x_copies:
        copy.wait()
    prefix = s_send[...]
    for d in range(3):
        prefix = prefix + jnp.where(d + 1 <= x, r_recv[d], 0.0)
    from_first = jnp.where(core == 0, s_own[...], s_recv[...])
    longer = prefix + from_first
    c_send[...] = jnp.where(core == 0, longer, prefix).astype(BF16)
    cross = remote(c_send, c_recv, c_sems.at[0], c_sems.at[1], partner)
    cross.start()
    c_own[...] = jnp.where(core == 0, prefix, longer).astype(BF16)
    c_blk[...] = jnp.zeros((WIDE, WIDE), BF16)
    loads[3].wait()
    cross.wait()
    mine, other = c_own[...].astype(F32), c_recv[...].astype(F32)
    c_blk[pl.ds(0, HD), pl.ds(0, HD)] = jnp.where(core == 0, mine, other).astype(BF16)
    c_blk[pl.ds(HD, HD), pl.ds(HD, HD)] = jnp.where(core == 0, other, mine).astype(BF16)

    def piece_at(owner, half):
        return mixed.at[owner, pl.ds(half * HALF, HALF)]

    def hop(owner, half, send, recv, step, where):
        ref = piece_at(owner, half)
        return remote(ref, ref, send.at[step], recv.at[step], where)

    def right_a(step):
        return hop((z + RING - step) % RING, 0, ra_send, ra_recv, step, right)

    def right_b(step):
        return hop((z + RING - step) % RING, 1, rb_send, rb_recv, step, right)

    def left_a(step):
        return hop((z + step) % RING, 0, la_send, la_recv, step, left)

    def left_b(step):
        return hop((z + step) % RING, 1, lb_send, lb_recv, step, left)

    def norm_half(half):
        for part in range(2):
            rows = pl.ds(half * HALF + part * SUB, SUB)
            attended = intra[rows, :] + dot(q[rows, :], c_blk[...])
            for head in range(2):
                own = attended[:, head * HD:(head + 1) * HD]
                scale = lax.rsqrt(jnp.mean(own * own, -1, keepdims=True) + 1e-06)
                mixed[z, rows, pl.ds(head * HD, HD)] = (own * scale).astype(BF16)

    norm_half(0)
    right_a(0).start()
    left_a(0).start()
    norm_half(1)
    left_b(0).start()
    right_b(0).start()

    def weights(owner):
        return w[pl.ds(pl.multiple_of(owner * WIDE, WIDE), WIDE), :]

    acc[...] = dot(mixed[z], weights(z))

    def add(owner, half):
        rows = pl.ds(half * HALF, HALF)
        acc[rows, :] += dot(mixed[owner, rows, :], weights(owner))

    def step_body(step, carry):
        before = (z + 2 * RING - step - 1) % RING
        after = (z + step + 1) % RING
        right_a(step).wait_recv()
        right_a(step + 1).start()
        left_b(step).wait_recv()
        left_b(step + 1).start()
        add(before, 0)
        add(after, 1)
        left_a(step).wait_recv()
        right_b(step).wait_recv()

        @pl.when(step < RING // 2 - 2)
        def _():
            left_a(step + 1).start()
            right_b(step + 1).start()

        add(after, 0)
        add(before, 1)
        return carry

    last = RING // 2 - 1
    lax.fori_loop(0, last, step_body, 0)
    far = (z + RING // 2) % RING
    for half, copy in ((0, right_a(last)), (1, left_b(last))):
        copy.wait_recv()
        rows = pl.ds(half * HALF, HALF)
        out[rows, :] = (acc[rows, :] + dot(mixed[far, rows, :], weights(far))).astype(BF16)

    def drain(step, carry):
        right_a(step).wait_send()
        left_b(step).wait_send()

        @pl.when(step < last)
        def _():
            left_a(step).wait_send()
            right_b(step).wait_send()

        return carry

    lax.fori_loop(0, last + 1, drain, 0)


def per_device(queries, keys, values, out_weight):
    dma = pltpu.SemaphoreType.DMA
    block = pltpu.VMEM((ROWS, WIDE), BF16)
    state = pltpu.VMEM((HD, HD), F32)
    small = pltpu.VMEM((HD, HD), BF16)
    scratch = [
        block, block, block, pltpu.VMEM((RING * WIDE, WIDE), BF16),
        pltpu.VMEM((ROWS, WIDE), F32), pltpu.VMEM((ROWS, WIDE), F32),
        pltpu.VMEM((RING, ROWS, WIDE), BF16),
        state, state, state, state, pltpu.VMEM((3, HD, HD), F32),
        state, pltpu.VMEM((3, HD, HD), F32),
        small, small, small, pltpu.VMEM((WIDE, WIDE), BF16),
        dma((4,)), dma, dma, dma((3,)), dma((3,)), dma((3,)), dma((3,)), dma((2,)),
    ] + [dma((RING // 2,))] * 8
    return pl.pallas_call(
        kernel,
        out_shape=jax.ShapeDtypeStruct((ROWS, WIDE), BF16),
        in_specs=[pl.BlockSpec(memory_space=pl.ANY)] * 4,
        out_specs=pl.BlockSpec(memory_space=pltpu.VMEM),
        scratch_shapes=scratch,
        compiler_params=pltpu.CompilerParams(
            collective_id=0, has_side_effects=True, vmem_limit_bytes=48 * 1024 * 1024
        ),
        name="prefix_ring",
    )(queries, keys, values, out_weight)


def solution(mesh):
    return jax.shard_map(
        per_device,
        mesh=mesh,
        in_specs=(P("seq", "head"), P("seq", "head"), P("seq", "head"), P(None, "head")),
        out_specs=P("seq", "head"),
        check_vma=False,
    )
```

```python
import jax
import jax.numpy as jnp
from jax import lax
from jax.experimental import pallas as pl
from jax.experimental.pallas import tpu as pltpu
from jax.sharding import PartitionSpec as P

HD = 128
ROWS = 1024
HALF = 512
WIDE = 256
SUB = 256
RING = 16
GROUP = 32
SHARE = 8
F32 = jnp.float32
BF16 = jnp.bfloat16


def dot(a, b):
    return jnp.dot(a, b, preferred_element_type=F32)


def remote(src, dst, send, recv, where):
    return pltpu.make_async_remote_copy(
        src_ref=src,
        dst_ref=dst,
        send_sem=send,
        recv_sem=recv,
        device_id=where,
        device_id_type=pl.DeviceIdType.MESH,
    )


def kernel(
    q_hbm, k_hbm, v_hbm, w_hbm, out,
    q, k, v, w, intra, acc, mixed,
    shares, gathered, sums, carried, c_blk,
    in_sems, s_send, s_recv, c_send, c_recv,
    ra_send, ra_recv, rb_send, rb_recv, la_send, la_recv, lb_send, lb_recv,
):
    seq, z = lax.axis_index("seq"), lax.axis_index("head")
    right = {"head": (z + 1) % RING}
    left = {"head": (z + RING - 1) % RING}

    barrier = pltpu.get_barrier_semaphore()

    def greet(who):
        pl.semaphore_signal(barrier, inc=1, device_id=who, device_id_type=pl.DeviceIdType.MESH)

    def greet_peer(ahead, carry):
        greet({"seq": (seq + ahead) % GROUP})
        return carry

    greet(right)
    greet(left)
    lax.fori_loop(1, GROUP, greet_peer, 0)
    loads = [
        pltpu.make_async_copy(src, dst, in_sems.at[i])
        for i, (src, dst) in enumerate(((k_hbm, k), (v_hbm, v), (q_hbm, q), (w_hbm, w)))
    ]
    for load in loads:
        load.start()
    loads[0].wait()
    loads[1].wait()
    states = lax.dot_general(k[...], v[...], (((0,), (0,)), ((), ())), preferred_element_type=F32)
    first, second = states[:HD, :HD], states[HD:, HD:]
    shares[pl.ds(0, GROUP // 2)] = states[:HD, :HD].reshape(GROUP // 2, SHARE, HD)
    shares[pl.ds(GROUP // 2, GROUP // 2)] = states[HD:, HD:].reshape(GROUP // 2, SHARE, HD)
    pl.semaphore_wait(barrier, GROUP + 1)

    def outgoing(ahead):
        peer = (seq + ahead) % GROUP
        return remote(
            shares.at[peer], gathered.at[seq], s_send.at[ahead], s_recv.at[ahead], {"seq": peer}
        )

    def returning(ahead):
        peer = (seq + ahead) % GROUP
        return remote(
            sums.at[peer], carried.at[seq], c_send.at[ahead], c_recv.at[ahead], {"seq": peer}
        )

    def start_all(copy):
        def body(ahead, carry):
            copy(ahead).start()
            return carry

        lax.fori_loop(1, GROUP, body, 0)

    def wait_all(copy):
        def body(ahead, carry):
            copy(ahead).wait()
            return carry

        lax.fori_loop(1, GROUP, body, 0)

    start_all(outgoing)
    gathered[seq] = shares[seq]

    def intra_part(head, part):
        cols = pl.ds(head * HD, HD)
        rows = pl.ds(part * SUB, SUB)
        width = (part + 1) * SUB
        scores = lax.dot_general(
            q[rows, cols], k[pl.ds(0, width), cols], (((1,), (1,)), ((), ())),
            preferred_element_type=F32,
        )
        query_at = lax.broadcasted_iota(jnp.int32, (SUB, width), 0) + part * SUB
        key_at = lax.broadcasted_iota(jnp.int32, (SUB, width), 1)
        scores = jnp.where(query_at >= key_at, scores, 0.0).astype(BF16)
        intra[rows, cols] = dot(scores, v[pl.ds(0, width), cols])

    loads[2].wait()
    for head in range(2):
        for part in range(2):
            intra_part(head, part)
    wait_all(outgoing)
    running = jnp.zeros((SHARE, HD), F32)
    for source in range(GROUP):
        sums[source] = running.astype(sums.dtype)
        running = running + gathered[source]
    start_all(returning)
    carried[seq] = sums[seq]
    c_blk[...] = jnp.zeros((WIDE, WIDE), BF16)
    intra_part(0, 2)
    intra_part(1, 2)
    loads[3].wait()
    wait_all(returning)
    for head in range(2):
        mine = carried[pl.ds(head * GROUP // 2, GROUP // 2)].astype(F32).reshape(HD, HD)
        c_blk[pl.ds(head * HD, HD), pl.ds(head * HD, HD)] = mine.astype(BF16)

    def piece_at(owner, half):
        return mixed.at[owner, pl.ds(half * HALF, HALF)]

    def hop(owner, half, send, recv, step, where):
        ref = piece_at(owner, half)
        return remote(ref, ref, send.at[step], recv.at[step], where)

    def right_a(step):
        return hop((z + RING - step) % RING, 0, ra_send, ra_recv, step, right)

    def right_b(step):
        return hop((z + RING - step) % RING, 1, rb_send, rb_recv, step, right)

    def left_a(step):
        return hop((z + step) % RING, 0, la_send, la_recv, step, left)

    def left_b(step):
        return hop((z + step) % RING, 1, lb_send, lb_recv, step, left)

    def norm_half(half):
        for part in range(2):
            rows = pl.ds(half * HALF + part * SUB, SUB)
            attended = intra[rows, :] + dot(q[rows, :], c_blk[...])
            for head in range(2):
                own = attended[:, head * HD:(head + 1) * HD]
                scale = lax.rsqrt(jnp.mean(own * own, -1, keepdims=True) + 1e-06)
                mixed[z, rows, pl.ds(head * HD, HD)] = (own * scale).astype(BF16)

    norm_half(0)
    right_a(0).start()
    left_a(0).start()
    intra_part(0, 3)
    intra_part(1, 3)
    norm_half(1)
    left_b(0).start()
    right_b(0).start()

    def weights(owner):
        return w[pl.ds(pl.multiple_of(owner * WIDE, WIDE), WIDE), :]

    acc[...] = dot(mixed[z], weights(z))

    def add(owner, half):
        rows = pl.ds(half * HALF, HALF)
        acc[rows, :] += dot(mixed[owner, rows, :], weights(owner))

    def step_body(step, carry):
        before = (z + 2 * RING - step - 1) % RING
        after = (z + step + 1) % RING
        right_a(step).wait_recv()
        right_a(step + 1).start()
        left_b(step).wait_recv()
        left_b(step + 1).start()
        add(before, 0)
        add(after, 1)
        left_a(step).wait_recv()
        right_b(step).wait_recv()

        @pl.when(step < RING // 2 - 2)
        def _():
            left_a(step + 1).start()
            right_b(step + 1).start()

        add(after, 0)
        add(before, 1)
        return carry

    last = RING // 2 - 1
    lax.fori_loop(0, last, step_body, 0)
    far = (z + RING // 2) % RING
    for half, copy in ((0, right_a(last)), (1, left_b(last))):
        copy.wait_recv()
        rows = pl.ds(half * HALF, HALF)
        out[rows, :] = (acc[rows, :] + dot(mixed[far, rows, :], weights(far))).astype(BF16)

    def drain(step, carry):
        right_a(step).wait_send()
        left_b(step).wait_send()

        @pl.when(step < last)
        def _():
            left_a(step).wait_send()
            right_b(step).wait_send()

        return carry

    lax.fori_loop(0, last + 1, drain, 0)


def per_device(queries, keys, values, out_weight):
    dma = pltpu.SemaphoreType.DMA
    block = pltpu.VMEM((ROWS, WIDE), BF16)
    share = pltpu.VMEM((GROUP, SHARE, HD), F32)
    small = pltpu.VMEM((GROUP, SHARE, HD), BF16)
    scratch = [
        block, block, block, pltpu.VMEM((RING * WIDE, WIDE), BF16),
        pltpu.VMEM((ROWS, WIDE), F32), pltpu.VMEM((ROWS, WIDE), F32),
        pltpu.VMEM((RING, ROWS, WIDE), BF16),
        share, share, small, small, pltpu.VMEM((WIDE, WIDE), BF16),
        dma((4,)), dma((GROUP,)), dma((GROUP,)), dma((GROUP,)), dma((GROUP,)),
    ] + [dma((RING // 2,))] * 8
    return pl.pallas_call(
        kernel,
        out_shape=jax.ShapeDtypeStruct((ROWS, WIDE), BF16),
        in_specs=[pl.BlockSpec(memory_space=pl.ANY)] * 4,
        out_specs=pl.BlockSpec(memory_space=pltpu.VMEM),
        scratch_shapes=scratch,
        compiler_params=pltpu.CompilerParams(
            collective_id=0, has_side_effects=True, vmem_limit_bytes=67_043_328
        ),
        name="prefix_ring",
    )(queries, keys, values, out_weight)


def solution(mesh):
    return jax.shard_map(
        per_device,
        mesh=mesh,
        in_specs=(P("seq", "head"), P("seq", "head"), P("seq", "head"), P(None, "head")),
        out_specs=P("seq", "head"),
        check_vma=False,
    )
```

```python
import jax
import jax.numpy as jnp
from jax import lax
from jax.experimental import pallas as pl
from jax.experimental.pallas import tpu as pltpu
from jax.sharding import PartitionSpec as P

HD = 128
ROWS = 1024
HALF = 512
WIDE = 256
SUB = 256
RING = 16
GROUP = 32
SHARE = 8
F32 = jnp.float32
BF16 = jnp.bfloat16


def dot(a, b):
    return jnp.dot(a, b, preferred_element_type=F32)


def remote(src, dst, send, recv, where):
    return pltpu.make_async_remote_copy(
        src_ref=src,
        dst_ref=dst,
        send_sem=send,
        recv_sem=recv,
        device_id=where,
        device_id_type=pl.DeviceIdType.MESH,
    )


def kernel(
    q_hbm, k_hbm, v_hbm, w_hbm, out,
    q, k, v, w, intra, acc, mixed,
    shares, gathered, sums, carried, c_blk,
    in_sems, s_send, s_recv, c_send, c_recv,
    ra_send, ra_recv, rb_send, rb_recv, la_send, la_recv, lb_send, lb_recv,
):
    seq, z = lax.axis_index("seq"), lax.axis_index("head")
    right = {"head": (z + 1) % RING}
    left = {"head": (z + RING - 1) % RING}

    barrier = pltpu.get_barrier_semaphore()

    def greet(who):
        pl.semaphore_signal(barrier, inc=1, device_id=who, device_id_type=pl.DeviceIdType.MESH)

    def greet_peer(ahead, carry):
        greet({"seq": (seq + ahead) % GROUP})
        return carry

    loads = [
        pltpu.make_async_copy(src, dst, in_sems.at[i])
        for i, (src, dst) in enumerate(((k_hbm, k), (v_hbm, v), (q_hbm, q), (w_hbm, w)))
    ]
    loads[0].start()
    loads[1].start()
    greet(right)
    greet(left)
    lax.fori_loop(1, GROUP, greet_peer, 0)
    loads[0].wait()
    loads[1].wait()
    loads[2].start()
    loads[3].start()
    states = lax.dot_general(k[...], v[...], (((0,), (0,)), ((), ())), preferred_element_type=F32)
    shares[pl.ds(0, GROUP // 2)] = states[:HD, :HD].reshape(GROUP // 2, SHARE, HD)
    shares[pl.ds(GROUP // 2, GROUP // 2)] = states[HD:, HD:].reshape(GROUP // 2, SHARE, HD)
    pl.semaphore_wait(barrier, GROUP + 1)

    def outgoing(ahead):
        peer = (seq + ahead) % GROUP
        return remote(
            shares.at[peer], gathered.at[seq], s_send.at[ahead], s_recv.at[ahead], {"seq": peer}
        )

    def returning(ahead):
        peer = (seq + ahead) % GROUP
        return remote(
            sums.at[peer], carried.at[seq], c_send.at[ahead], c_recv.at[ahead], {"seq": peer}
        )

    def start_all(copy):
        def body(ahead, carry):
            copy(ahead).start()
            return carry

        lax.fori_loop(1, GROUP, body, 0)

    def wait_all(copy):
        def body(ahead, carry):
            copy(ahead).wait()
            return carry

        lax.fori_loop(1, GROUP, body, 0)

    start_all(outgoing)
    gathered[seq] = shares[seq]

    def intra_part(head, part):
        cols = pl.ds(head * HD, HD)
        rows = pl.ds(part * SUB, SUB)
        width = (part + 1) * SUB
        scores = lax.dot_general(
            q[rows, cols], k[pl.ds(0, width), cols], (((1,), (1,)), ((), ())),
            preferred_element_type=F32,
        )
        query_at = lax.broadcasted_iota(jnp.int32, (SUB, width), 0) + part * SUB
        key_at = lax.broadcasted_iota(jnp.int32, (SUB, width), 1)
        scores = jnp.where(query_at >= key_at, scores, 0.0).astype(BF16)
        intra[rows, cols] = dot(scores, v[pl.ds(0, width), cols])

    loads[2].wait()
    for head in range(2):
        for part in range(2):
            intra_part(head, part)
    wait_all(outgoing)
    running = jnp.zeros((SHARE, HD), F32)
    for source in range(GROUP):
        sums[source] = running.astype(sums.dtype)
        running = running + gathered[source]
    start_all(returning)
    carried[seq] = sums[seq]
    c_blk[...] = jnp.zeros((WIDE, WIDE), BF16)
    intra_part(0, 2)
    intra_part(1, 2)
    loads[3].wait()
    wait_all(returning)
    for head in range(2):
        mine = carried[pl.ds(head * GROUP // 2, GROUP // 2)].astype(F32).reshape(HD, HD)
        c_blk[pl.ds(head * HD, HD), pl.ds(head * HD, HD)] = mine.astype(BF16)

    def piece_at(owner, half):
        return mixed.at[owner, pl.ds(half * HALF, HALF)]

    def hop(owner, half, send, recv, step, where):
        ref = piece_at(owner, half)
        return remote(ref, ref, send.at[step], recv.at[step], where)

    def right_a(step):
        return hop((z + RING - step) % RING, 0, ra_send, ra_recv, step, right)

    def right_b(step):
        return hop((z + RING - step) % RING, 1, rb_send, rb_recv, step, right)

    def left_a(step):
        return hop((z + step) % RING, 0, la_send, la_recv, step, left)

    def left_b(step):
        return hop((z + step) % RING, 1, lb_send, lb_recv, step, left)

    def norm_half(half):
        for part in range(2):
            rows = pl.ds(half * HALF + part * SUB, SUB)
            attended = intra[rows, :] + dot(q[rows, :], c_blk[...])
            for head in range(2):
                own = attended[:, head * HD:(head + 1) * HD]
                scale = lax.rsqrt(jnp.mean(own * own, -1, keepdims=True) + 1e-06)
                mixed[z, rows, pl.ds(head * HD, HD)] = (own * scale).astype(BF16)

    norm_half(0)
    right_a(0).start()
    left_a(0).start()
    intra_part(0, 3)
    intra_part(1, 3)
    norm_half(1)
    left_b(0).start()
    right_b(0).start()

    def weights(owner):
        return w[pl.ds(pl.multiple_of(owner * WIDE, WIDE), WIDE), :]

    acc[...] = dot(mixed[z], weights(z))

    def add(owner, half):
        rows = pl.ds(half * HALF, HALF)
        acc[rows, :] += dot(mixed[owner, rows, :], weights(owner))

    def step_body(step, carry):
        before = (z + 2 * RING - step - 1) % RING
        after = (z + step + 1) % RING
        right_a(step).wait_recv()
        right_a(step + 1).start()
        left_b(step).wait_recv()
        left_b(step + 1).start()
        add(before, 0)
        add(after, 1)
        left_a(step).wait_recv()
        right_b(step).wait_recv()

        @pl.when(step < RING // 2 - 2)
        def _():
            left_a(step + 1).start()
            right_b(step + 1).start()

        add(after, 0)
        add(before, 1)
        return carry

    last = RING // 2 - 1
    lax.fori_loop(0, last, step_body, 0)
    far = (z + RING // 2) % RING
    for half, copy in ((0, right_a(last)), (1, left_b(last))):
        copy.wait_recv()
        rows = pl.ds(half * HALF, HALF)
        out[rows, :] = (acc[rows, :] + dot(mixed[far, rows, :], weights(far))).astype(BF16)

    def drain(step, carry):
        right_a(step).wait_send()
        left_b(step).wait_send()

        @pl.when(step < last)
        def _():
            left_a(step).wait_send()
            right_b(step).wait_send()

        return carry

    lax.fori_loop(0, last + 1, drain, 0)


def per_device(queries, keys, values, out_weight):
    dma = pltpu.SemaphoreType.DMA
    block = pltpu.VMEM((ROWS, WIDE), BF16)
    share = pltpu.VMEM((GROUP, SHARE, HD), F32)
    small = pltpu.VMEM((GROUP, SHARE, HD), BF16)
    scratch = [
        block, block, block, pltpu.VMEM((RING * WIDE, WIDE), BF16),
        pltpu.VMEM((ROWS, WIDE), F32), pltpu.VMEM((ROWS, WIDE), F32),
        pltpu.VMEM((RING, ROWS, WIDE), BF16),
        share, share, small, small, pltpu.VMEM((WIDE, WIDE), BF16),
        dma((4,)), dma((GROUP,)), dma((GROUP,)), dma((GROUP,)), dma((GROUP,)),
    ] + [dma((RING // 2,))] * 8
    return pl.pallas_call(
        kernel,
        out_shape=jax.ShapeDtypeStruct((ROWS, WIDE), BF16),
        in_specs=[pl.BlockSpec(memory_space=pltpu.HBM)] * 4,
        out_specs=pl.BlockSpec(memory_space=pltpu.VMEM),
        scratch_shapes=scratch,
        compiler_params=pltpu.CompilerParams(
            collective_id=0, has_side_effects=True, vmem_limit_bytes=32 * 1024 * 1024
        ),
        name="prefix_ring",
    )(*(pltpu.with_memory_space_constraint(a, pltpu.HBM) for a in (queries, keys, values, out_weight)))


def solution(mesh):
    return jax.shard_map(
        per_device,
        mesh=mesh,
        in_specs=(P("seq", "head"), P("seq", "head"), P("seq", "head"), P(None, "head")),
        out_specs=P("seq", "head"),
        check_vma=False,
    )
```

```python
import jax
import jax.numpy as jnp
from jax import lax
from jax.experimental import pallas as pl
from jax.experimental.pallas import tpu as pltpu
from jax.sharding import PartitionSpec as P

HD = 128
ROWS = 1024
HALF = 512
WIDE = 256
SUB = 256
RING = 16
GROUP = 32
SHARE = 8
F32 = jnp.float32
BF16 = jnp.bfloat16


def dot(a, b):
    return jnp.dot(a, b, preferred_element_type=F32)


def remote(src, dst, send, recv, where):
    return pltpu.make_async_remote_copy(
        src_ref=src,
        dst_ref=dst,
        send_sem=send,
        recv_sem=recv,
        device_id=where,
        device_id_type=pl.DeviceIdType.MESH,
    )


def kernel(
    q_hbm, k_hbm, v_hbm, w_hbm, out,
    q, k, v, w, intra, acc, mixed,
    shares, gathered, sums, carried, c_blk,
    in_sems, s_send, s_recv, c_send, c_recv,
    r_send, r_recv, l_send, l_recv,
):
    seq, z = lax.axis_index("seq"), lax.axis_index("head")
    right = {"head": (z + 1) % RING}
    left = {"head": (z + RING - 1) % RING}

    barrier = pltpu.get_barrier_semaphore()

    def greet(who):
        pl.semaphore_signal(barrier, inc=1, device_id=who, device_id_type=pl.DeviceIdType.MESH)

    def greet_peer(ahead, carry):
        greet({"seq": (seq + ahead) % GROUP})
        return carry

    loads = [
        pltpu.make_async_copy(src, dst, in_sems.at[i])
        for i, (src, dst) in enumerate(((k_hbm, k), (v_hbm, v), (q_hbm, q), (w_hbm, w)))
    ]
    loads[0].start()
    loads[1].start()
    greet(right)
    greet(left)
    lax.fori_loop(1, GROUP, greet_peer, 0)
    loads[0].wait()
    loads[1].wait()
    loads[2].start()
    loads[3].start()
    states = lax.dot_general(k[...], v[...], (((0,), (0,)), ((), ())), preferred_element_type=F32)
    shares[pl.ds(0, GROUP // 2)] = states[:HD, :HD].reshape(GROUP // 2, SHARE, HD)
    shares[pl.ds(GROUP // 2, GROUP // 2)] = states[HD:, HD:].reshape(GROUP // 2, SHARE, HD)
    pl.semaphore_wait(barrier, GROUP + 1)

    def outgoing(ahead):
        peer = (seq + ahead) % GROUP
        return remote(
            shares.at[peer], gathered.at[seq], s_send.at[ahead], s_recv.at[ahead], {"seq": peer}
        )

    def returning(ahead):
        peer = (seq + ahead) % GROUP
        return remote(
            sums.at[peer], carried.at[seq], c_send.at[ahead], c_recv.at[ahead], {"seq": peer}
        )

    def start_all(copy):
        def body(ahead, carry):
            copy(ahead).start()
            return carry

        lax.fori_loop(1, GROUP, body, 0)

    def wait_all(copy):
        def body(ahead, carry):
            copy(ahead).wait()
            return carry

        lax.fori_loop(1, GROUP, body, 0)

    start_all(outgoing)
    gathered[seq] = shares[seq]

    def intra_part(head, part):
        cols = pl.ds(head * HD, HD)
        rows = pl.ds(part * SUB, SUB)
        width = (part + 1) * SUB
        scores = lax.dot_general(
            q[rows, cols], k[pl.ds(0, width), cols], (((1,), (1,)), ((), ())),
            preferred_element_type=F32,
        )
        query_at = lax.broadcasted_iota(jnp.int32, (SUB, width), 0) + part * SUB
        key_at = lax.broadcasted_iota(jnp.int32, (SUB, width), 1)
        scores = jnp.where(query_at >= key_at, scores, 0.0).astype(BF16)
        intra[rows, cols] = dot(scores, v[pl.ds(0, width), cols])

    loads[2].wait()
    for head in range(2):
        for part in range(2):
            intra_part(head, part)
    wait_all(outgoing)
    running = jnp.zeros((SHARE, HD), F32)
    for source in range(GROUP):
        sums[source] = running.astype(sums.dtype)
        running = running + gathered[source]
    start_all(returning)
    carried[seq] = sums[seq]
    c_blk[...] = jnp.zeros((WIDE, WIDE), BF16)
    intra_part(0, 2)
    intra_part(1, 2)
    loads[3].wait()
    wait_all(returning)
    for head in range(2):
        mine = carried[pl.ds(head * GROUP // 2, GROUP // 2)].astype(F32).reshape(HD, HD)
        c_blk[pl.ds(head * HD, HD), pl.ds(head * HD, HD)] = mine.astype(BF16)

    def to_right(part, step):
        ref = mixed.at[(z + RING - step) % RING, pl.ds(part * SUB, SUB)]
        return remote(ref, ref, r_send.at[part, step], r_recv.at[part, step], right)

    def to_left(part, step):
        ref = mixed.at[(z + step) % RING, pl.ds(part * SUB, SUB)]
        return remote(ref, ref, l_send.at[part, step], l_recv.at[part, step], left)

    for part in range(4):
        if part == 3:
            intra_part(0, 3)
            intra_part(1, 3)
        rows = pl.ds(part * SUB, SUB)
        attended = intra[rows, :] + dot(q[rows, :], c_blk[...])
        for head in range(2):
            own = attended[:, head * HD:(head + 1) * HD]
            scale = lax.rsqrt(jnp.mean(own * own, -1, keepdims=True) + 1e-06)
            mixed[z, rows, pl.ds(head * HD, HD)] = (own * scale).astype(BF16)
        to_right(part, 0).start()
        to_left(part, 0).start()

    def weights(owner):
        return w[pl.ds(pl.multiple_of(owner * WIDE, WIDE), WIDE), :]

    acc[...] = dot(mixed[z], weights(z))

    def add(owner, half):
        rows = pl.ds(half * HALF, HALF)
        acc[rows, :] += dot(mixed[owner, rows, :], weights(owner))

    far_pieces = ((to_right, 0), (to_left, 2), (to_right, 1), (to_left, 3))
    near_pieces = ((to_left, 0), (to_right, 2), (to_left, 1), (to_right, 3))
    last = RING // 2 - 1

    def step_body(step, carry):
        before = (z + 2 * RING - step - 1) % RING
        after = (z + step + 1) % RING
        for copy, part in far_pieces:
            copy(part, step).wait_recv()
            copy(part, step + 1).start()
        add(before, 0)
        add(after, 1)
        for copy, part in near_pieces:
            copy(part, step).wait_recv()

            @pl.when(step < last - 1)
            def _():
                copy(part, step + 1).start()

        add(after, 0)
        add(before, 1)
        return carry

    lax.fori_loop(0, last, step_body, 0)
    far = (z + RING // 2) % RING
    for copy, part in far_pieces:
        copy(part, last).wait_recv()
        rows = pl.ds(part * SUB, SUB)
        out[rows, :] = (acc[rows, :] + dot(mixed[far, rows, :], weights(far))).astype(BF16)

    def drain(step, carry):
        for copy, part in far_pieces:
            copy(part, step).wait_send()

        @pl.when(step < last)
        def _():
            for copy, part in near_pieces:
                copy(part, step).wait_send()

        return carry

    lax.fori_loop(0, last + 1, drain, 0)


def per_device(queries, keys, values, out_weight):
    dma = pltpu.SemaphoreType.DMA
    block = pltpu.VMEM((ROWS, WIDE), BF16)
    share = pltpu.VMEM((GROUP, SHARE, HD), F32)
    small = pltpu.VMEM((GROUP, SHARE, HD), BF16)
    scratch = [
        block, block, block, pltpu.VMEM((RING * WIDE, WIDE), BF16),
        pltpu.VMEM((ROWS, WIDE), F32), pltpu.VMEM((ROWS, WIDE), F32),
        pltpu.VMEM((RING, ROWS, WIDE), BF16),
        share, share, small, small, pltpu.VMEM((WIDE, WIDE), BF16),
        dma((4,)), dma((GROUP,)), dma((GROUP,)), dma((GROUP,)), dma((GROUP,)),
    ] + [dma((4, RING // 2))] * 4
    return pl.pallas_call(
        kernel,
        out_shape=jax.ShapeDtypeStruct((ROWS, WIDE), BF16),
        in_specs=[pl.BlockSpec(memory_space=pltpu.HBM)] * 4,
        out_specs=pl.BlockSpec(memory_space=pltpu.VMEM),
        scratch_shapes=scratch,
        compiler_params=pltpu.CompilerParams(
            collective_id=0, has_side_effects=True, vmem_limit_bytes=32 * 1024 * 1024
        ),
        name="prefix_ring",
    )(*(pltpu.with_memory_space_constraint(a, pltpu.HBM) for a in (queries, keys, values, out_weight)))


def solution(mesh):
    return jax.shard_map(
        per_device,
        mesh=mesh,
        in_specs=(P("seq", "head"), P("seq", "head"), P("seq", "head"), P(None, "head")),
        out_specs=P("seq", "head"),
        check_vma=False,
    )
```

```python
import jax
import jax.numpy as jnp
from jax import lax
from jax.experimental import pallas as pl
from jax.experimental.pallas import tpu as pltpu
from jax.sharding import PartitionSpec as P

HD = 128
ROWS = 1024
HALF = 512
WIDE = 256
SUB = 256
RING = 16
GROUP = 32
SHARE = 8
F32 = jnp.float32
BF16 = jnp.bfloat16


def dot(a, b):
    return jnp.dot(a, b, preferred_element_type=F32)


def remote(src, dst, send, recv, where):
    return pltpu.make_async_remote_copy(
        src_ref=src,
        dst_ref=dst,
        send_sem=send,
        recv_sem=recv,
        device_id=where,
        device_id_type=pl.DeviceIdType.MESH,
    )


def kernel(
    q_hbm, k_hbm, v_hbm, w_hbm, out,
    q, k, v, w, intra, acc, mixed,
    shares, gathered, sums, carried, c_blk,
    in_sems, s_send, s_recv, c_send, c_recv,
    r_send, r_recv,
):
    seq, z = lax.axis_index("seq"), lax.axis_index("head")
    right = {"head": (z + 1) % RING}
    left = {"head": (z + RING - 1) % RING}

    barrier = pltpu.get_barrier_semaphore()

    def greet(who):
        pl.semaphore_signal(barrier, inc=1, device_id=who, device_id_type=pl.DeviceIdType.MESH)

    def greet_peer(ahead, carry):
        greet({"seq": (seq + ahead) % GROUP})
        return carry

    loads = [
        pltpu.make_async_copy(src, dst, in_sems.at[i])
        for i, (src, dst) in enumerate(((k_hbm, k), (v_hbm, v), (q_hbm, q), (w_hbm, w)))
    ]
    loads[0].start()
    loads[1].start()
    greet(right)
    greet(left)
    lax.fori_loop(1, GROUP, greet_peer, 0)
    loads[0].wait()
    loads[1].wait()
    loads[2].start()
    loads[3].start()
    states = lax.dot_general(k[...], v[...], (((0,), (0,)), ((), ())), preferred_element_type=F32)
    shares[pl.ds(0, GROUP // 2)] = states[:HD, :HD].reshape(GROUP // 2, SHARE, HD)
    shares[pl.ds(GROUP // 2, GROUP // 2)] = states[HD:, HD:].reshape(GROUP // 2, SHARE, HD)
    pl.semaphore_wait(barrier, GROUP + 1)

    def outgoing(ahead):
        peer = (seq + ahead) % GROUP
        return remote(
            shares.at[peer], gathered.at[seq], s_send.at[ahead], s_recv.at[ahead], {"seq": peer}
        )

    def returning(ahead):
        peer = (seq + ahead) % GROUP
        return remote(
            sums.at[peer], carried.at[seq], c_send.at[ahead], c_recv.at[ahead], {"seq": peer}
        )

    def start_all(copy):
        def body(ahead, carry):
            copy(ahead).start()
            return carry

        lax.fori_loop(1, GROUP, body, 0)

    def wait_all(copy):
        def body(ahead, carry):
            copy(ahead).wait()
            return carry

        lax.fori_loop(1, GROUP, body, 0)

    start_all(outgoing)
    gathered[seq] = shares[seq]

    def intra_part(head, part):
        cols = pl.ds(head * HD, HD)
        rows = pl.ds(part * SUB, SUB)
        width = (part + 1) * SUB
        scores = lax.dot_general(
            q[rows, cols], k[pl.ds(0, width), cols], (((1,), (1,)), ((), ())),
            preferred_element_type=F32,
        )
        query_at = lax.broadcasted_iota(jnp.int32, (SUB, width), 0) + part * SUB
        key_at = lax.broadcasted_iota(jnp.int32, (SUB, width), 1)
        scores = jnp.where(query_at >= key_at, scores, 0.0).astype(BF16)
        intra[rows, cols] = dot(scores, v[pl.ds(0, width), cols])

    loads[2].wait()
    for head in range(2):
        for part in range(2):
            intra_part(head, part)
    wait_all(outgoing)
    running = jnp.zeros((SHARE, HD), F32)
    for source in range(GROUP):
        sums[source] = running.astype(sums.dtype)
        running = running + gathered[source]
    start_all(returning)
    carried[seq] = sums[seq]
    c_blk[...] = jnp.zeros((WIDE, WIDE), BF16)
    intra_part(0, 2)
    intra_part(1, 2)
    loads[3].wait()
    wait_all(returning)
    for head in range(2):
        mine = carried[pl.ds(head * GROUP // 2, GROUP // 2)].astype(F32).reshape(HD, HD)
        c_blk[pl.ds(head * HD, HD), pl.ds(head * HD, HD)] = mine.astype(BF16)

    core = seq % 2
    onward = {"head": (z + 1 + core * (RING - 2)) % RING}

    def owner_at(step):
        return (z + 2 * RING + step * (2 * core - 1)) % RING

    def piece(part, step):
        ref = mixed.at[owner_at(step), pl.ds(part * SUB, SUB)]
        return remote(ref, ref, r_send.at[part, step], r_recv.at[part, step], onward)

    for part in range(4):
        if part == 3:
            intra_part(0, 3)
            intra_part(1, 3)
        rows = pl.ds(part * SUB, SUB)
        attended = intra[rows, :] + dot(q[rows, :], c_blk[...])
        for head in range(2):
            own = attended[:, head * HD:(head + 1) * HD]
            scale = lax.rsqrt(jnp.mean(own * own, -1, keepdims=True) + 1e-06)
            mixed[z, rows, pl.ds(head * HD, HD)] = (own * scale).astype(BF16)
        piece(part, 0).start()

    def weights(owner):
        return w[pl.ds(pl.multiple_of(owner * WIDE, WIDE), WIDE), :]

    acc[...] = dot(mixed[z], weights(z))

    def add(owner, half):
        rows = pl.ds(half * HALF, HALF)
        acc[rows, :] += dot(mixed[owner, rows, :], weights(owner))

    last = RING - 2

    def step_body(step, carry):
        owner = owner_at(step + 1)
        for half in range(2):
            for part in (2 * half, 2 * half + 1):
                piece(part, step).wait_recv()
                piece(part, step + 1).start()
            add(owner, half)
        return carry

    lax.fori_loop(0, last, step_body, 0)
    far = owner_at(RING - 1)
    for part in range(4):
        piece(part, last).wait_recv()
        rows = pl.ds(part * SUB, SUB)
        out[rows, :] = (acc[rows, :] + dot(mixed[far, rows, :], weights(far))).astype(BF16)

    def drain(step, carry):
        for part in range(4):
            piece(part, step).wait_send()
        return carry

    lax.fori_loop(0, last + 1, drain, 0)


def per_device(queries, keys, values, out_weight):
    dma = pltpu.SemaphoreType.DMA
    block = pltpu.VMEM((ROWS, WIDE), BF16)
    share = pltpu.VMEM((GROUP, SHARE, HD), F32)
    small = pltpu.VMEM((GROUP, SHARE, HD), BF16)
    scratch = [
        block, block, block, pltpu.VMEM((RING * WIDE, WIDE), BF16),
        pltpu.VMEM((ROWS, WIDE), F32), pltpu.VMEM((ROWS, WIDE), F32),
        pltpu.VMEM((RING, ROWS, WIDE), BF16),
        share, share, small, small, pltpu.VMEM((WIDE, WIDE), BF16),
        dma((4,)), dma((GROUP,)), dma((GROUP,)), dma((GROUP,)), dma((GROUP,)),
    ] + [dma((4, RING - 1))] * 2
    return pl.pallas_call(
        kernel,
        out_shape=jax.ShapeDtypeStruct((ROWS, WIDE), BF16),
        in_specs=[pl.BlockSpec(memory_space=pltpu.HBM)] * 4,
        out_specs=pl.BlockSpec(memory_space=pltpu.VMEM),
        scratch_shapes=scratch,
        compiler_params=pltpu.CompilerParams(
            collective_id=0, has_side_effects=True, vmem_limit_bytes=32 * 1024 * 1024
        ),
        name="prefix_ring",
    )(*(pltpu.with_memory_space_constraint(a, pltpu.HBM) for a in (queries, keys, values, out_weight)))


def solution(mesh):
    return jax.shard_map(
        per_device,
        mesh=mesh,
        in_specs=(P("seq", "head"), P("seq", "head"), P("seq", "head"), P(None, "head")),
        out_specs=P("seq", "head"),
        check_vma=False,
    )
```

```python
import jax
import jax.numpy as jnp
from jax import lax
from jax.experimental import pallas as pl
from jax.experimental.pallas import tpu as pltpu
from jax.sharding import PartitionSpec as P

HD = 128
ROWS = 1024
HALF = 512
WIDE = 256
SUB = 256
RING = 16
GROUP = 32
SHARE = 8
F32 = jnp.float32
BF16 = jnp.bfloat16


def dot(a, b):
    return jnp.dot(a, b, preferred_element_type=F32)


def remote(src, dst, send, recv, where):
    return pltpu.make_async_remote_copy(
        src_ref=src,
        dst_ref=dst,
        send_sem=send,
        recv_sem=recv,
        device_id=where,
        device_id_type=pl.DeviceIdType.MESH,
    )


def kernel(
    q_hbm, k_hbm, v_hbm, w_hbm, out,
    q, k, v, w, intra, acc, mixed,
    shares, gathered, sums, carried, c_blk,
    in_sems, s_send, s_recv, c_send, c_recv,
    ra_send, ra_recv, rb_send, rb_recv, la_send, la_recv, lb_send, lb_recv,
):
    seq, z = lax.axis_index("seq"), lax.axis_index("head")
    right = {"head": (z + 1) % RING}
    left = {"head": (z + RING - 1) % RING}

    barrier = pltpu.get_barrier_semaphore()

    def greet(who):
        pl.semaphore_signal(barrier, inc=1, device_id=who, device_id_type=pl.DeviceIdType.MESH)

    def greet_peer(ahead, carry):
        greet({"seq": (seq + ahead) % GROUP})
        return carry

    loads = [
        pltpu.make_async_copy(src, dst, in_sems.at[i])
        for i, (src, dst) in enumerate(((k_hbm, k), (v_hbm, v), (q_hbm, q), (w_hbm, w)))
    ]
    loads[0].start()
    loads[1].start()
    greet(right)
    greet(left)
    lax.fori_loop(1, GROUP, greet_peer, 0)
    loads[0].wait()
    loads[1].wait()
    loads[2].start()
    loads[3].start()
    states = lax.dot_general(k[...], v[...], (((0,), (0,)), ((), ())), preferred_element_type=F32)
    shares[pl.ds(0, GROUP // 2)] = states[:HD, :HD].reshape(GROUP // 2, SHARE, HD)
    shares[pl.ds(GROUP // 2, GROUP // 2)] = states[HD:, HD:].reshape(GROUP // 2, SHARE, HD)
    pl.semaphore_wait(barrier, GROUP + 1)

    def outgoing(ahead):
        peer = (seq + ahead) % GROUP
        return remote(
            shares.at[peer], gathered.at[seq], s_send.at[ahead], s_recv.at[ahead], {"seq": peer}
        )

    def returning(ahead):
        peer = (seq + ahead) % GROUP
        return remote(
            sums.at[peer], carried.at[seq], c_send.at[ahead], c_recv.at[ahead], {"seq": peer}
        )

    def start_all(copy):
        def body(ahead, carry):
            copy(ahead).start()
            return carry

        lax.fori_loop(1, GROUP, body, 0)

    def wait_all(copy):
        def body(ahead, carry):
            copy(ahead).wait()
            return carry

        lax.fori_loop(1, GROUP, body, 0)

    start_all(outgoing)
    gathered[seq] = shares[seq]

    def intra_part(head, part):
        cols = pl.ds(head * HD, HD)
        rows = pl.ds(part * SUB, SUB)
        width = (part + 1) * SUB
        scores = lax.dot_general(
            q[rows, cols], k[pl.ds(0, width), cols], (((1,), (1,)), ((), ())),
            preferred_element_type=F32,
        )
        query_at = lax.broadcasted_iota(jnp.int32, (SUB, width), 0) + part * SUB
        key_at = lax.broadcasted_iota(jnp.int32, (SUB, width), 1)
        scores = jnp.where(query_at >= key_at, scores, 0.0).astype(BF16)
        intra[rows, cols] = dot(scores, v[pl.ds(0, width), cols])

    loads[2].wait()
    for head in range(2):
        for part in range(2):
            intra_part(head, part)
    wait_all(outgoing)
    running = jnp.zeros((SHARE, HD), F32)
    for source in range(GROUP):
        sums[source] = running.astype(sums.dtype)
        running = running + gathered[source]
    start_all(returning)
    carried[seq] = sums[seq]
    c_blk[...] = jnp.zeros((WIDE, WIDE), BF16)
    intra_part(0, 2)
    intra_part(1, 2)
    loads[3].wait()
    wait_all(returning)
    for head in range(2):
        mine = carried[pl.ds(head * GROUP // 2, GROUP // 2)].astype(F32).reshape(HD, HD)
        c_blk[pl.ds(head * HD, HD), pl.ds(head * HD, HD)] = mine.astype(BF16)

    def piece_at(owner, half):
        return mixed.at[owner, pl.ds(half * HALF, HALF)]

    def hop(owner, half, send, recv, step, where):
        ref = piece_at(owner, half)
        return remote(ref, ref, send.at[step], recv.at[step], where)

    def right_a(step):
        return hop((z + RING - step) % RING, 0, ra_send, ra_recv, step, right)

    def right_b(step):
        return hop((z + RING - step) % RING, 1, rb_send, rb_recv, step, right)

    def left_a(step):
        return hop((z + step) % RING, 0, la_send, la_recv, step, left)

    def left_b(step):
        return hop((z + step) % RING, 1, lb_send, lb_recv, step, left)

    def norm_half(half):
        for part in range(2):
            rows = pl.ds(half * HALF + part * SUB, SUB)
            attended = intra[rows, :] + dot(q[rows, :], c_blk[...])
            for head in range(2):
                own = attended[:, head * HD:(head + 1) * HD]
                scale = lax.rsqrt(jnp.mean(own * own, -1, keepdims=True) + 1e-06)
                mixed[z, rows, pl.ds(head * HD, HD)] = (own * scale).astype(BF16)

    norm_half(0)
    right_a(0).start()
    left_a(0).start()
    intra_part(0, 3)
    intra_part(1, 3)
    norm_half(1)
    left_b(0).start()
    right_b(0).start()

    def weights(owner):
        return w[pl.ds(pl.multiple_of(owner * WIDE, WIDE), WIDE), :]

    acc[...] = dot(mixed[z], weights(z))

    def add(owner, half):
        rows = pl.ds(half * HALF, HALF)
        acc[rows, :] += dot(mixed[owner, rows, :], weights(owner))

    def step_body(step, carry):
        before = (z + 2 * RING - step - 1) % RING
        after = (z + step + 1) % RING
        right_a(step).wait_recv()
        right_a(step + 1).start()
        left_b(step).wait_recv()
        left_b(step + 1).start()
        add(before, 0)
        add(after, 1)
        left_a(step).wait_recv()
        right_b(step).wait_recv()

        @pl.when(step < RING // 2 - 2)
        def _():
            left_a(step + 1).start()
            right_b(step + 1).start()

        add(after, 0)
        add(before, 1)

        @pl.when(step > 0)
        def _():
            for copy in (right_a, left_b, left_a, right_b):
                copy(step - 1).wait_send()

        return carry

    last = RING // 2 - 1
    lax.fori_loop(0, last, step_body, 0)
    for copy in (right_a, left_b, left_a, right_b):
        copy(last - 1).wait_send()
    far = (z + RING // 2) % RING
    for half, copy in ((0, right_a(last)), (1, left_b(last))):
        copy.wait_recv()
        rows = pl.ds(half * HALF, HALF)
        out[rows, :] = (acc[rows, :] + dot(mixed[far, rows, :], weights(far))).astype(BF16)

    right_a(last).wait_send()
    left_b(last).wait_send()


def per_device(queries, keys, values, out_weight):
    dma = pltpu.SemaphoreType.DMA
    block = pltpu.VMEM((ROWS, WIDE), BF16)
    share = pltpu.VMEM((GROUP, SHARE, HD), F32)
    small = pltpu.VMEM((GROUP, SHARE, HD), BF16)
    scratch = [
        block, block, block, pltpu.VMEM((RING * WIDE, WIDE), BF16),
        pltpu.VMEM((ROWS, WIDE), F32), pltpu.VMEM((ROWS, WIDE), F32),
        pltpu.VMEM((RING, ROWS, WIDE), BF16),
        share, share, small, small, pltpu.VMEM((WIDE, WIDE), BF16),
        dma((4,)), dma((GROUP,)), dma((GROUP,)), dma((GROUP,)), dma((GROUP,)),
    ] + [dma((RING // 2,))] * 8
    return pl.pallas_call(
        kernel,
        out_shape=jax.ShapeDtypeStruct((ROWS, WIDE), BF16),
        in_specs=[pl.BlockSpec(memory_space=pltpu.HBM)] * 4,
        out_specs=pl.BlockSpec(memory_space=pltpu.VMEM),
        scratch_shapes=scratch,
        compiler_params=pltpu.CompilerParams(
            collective_id=0, has_side_effects=True, vmem_limit_bytes=32 * 1024 * 1024
        ),
        name="prefix_ring",
    )(*(pltpu.with_memory_space_constraint(a, pltpu.HBM) for a in (queries, keys, values, out_weight)))


def solution(mesh):
    return jax.shard_map(
        per_device,
        mesh=mesh,
        in_specs=(P("seq", "head"), P("seq", "head"), P("seq", "head"), P(None, "head")),
        out_specs=P("seq", "head"),
        check_vma=False,
    )
```
